32 devices in a mesh: groups: 2 (over x), tm: 16 (over z, y, core).
Axes of the slice: x: 2, y: 2, z: 4, core: 2. Of those that a mesh axis runs over, the one named last changes fastest.
Arguments:
- pixels: bfloat16 [128, 128, 1536], P(('groups', 'tm')), parts along dimension 0, as said below
- prior_kv: bfloat16 [2, 16, 128, 640], P(None, 'groups'), parts along dimension 1, may hold values from -6 to 6
- w_embed: bfloat16 [1536, 1280], replicated, may hold values from -0.15625 to 0.15625
- ln_gain: float32 [1280], replicated, may hold values from 0.1 to 1.9
- w_query: bfloat16 [1280, 640], replicated, as said below
- w_key: bfloat16 [1280, 640], replicated, as said below
- w_value: bfloat16 [1280, 640], replicated, may hold values from -0.15625 to 0.15625
- w_out: bfloat16 [640, 1280], replicated, may hold values from -0.25 to 0.25
Outputs:
- encoded: bfloat16 [128, 128, 1280], P(('groups', 'tm')), parts along dimension 0
The draws below stay inside these ranges and needn't reach their ends.
There are 2 independent parts, one for each index of `groups`. The reference program is written for one: setup_inputs(seed, part) draws one part's arguments, and reference() takes and returns one part's arrays. A program takes and returns all parts, laid end to end along the dimension named above; an argument that names none is the same for every part. Nothing has to cross between parts.
Inputs may be any that keep to these rules, and one draw needn't show every extreme that they name: `pixels`: standardized pixel values. `w_query`: query projection, entries of order 1280 ** -0.5. `w_key`: key projection.
All inputs are finite; a program needn't handle non-finite values.
Results may differ from the reference program's by a relative error of at most 0.007.
Values may be sent and summed in bfloat16 or wider, within the bound.
A program may use at most 64 MiB of HBM per device.

```python
import math
import jax
import jax.numpy as jnp
from jax import lax

D = 1280
HEADS = 8
HEAD_DIM = 80
PIX = 1536
P_SIZE = 128
TUBELETS = 64
WINDOW = 8


def shared_matrix(key):
    return jax.random.truncated_normal(jax.random.fold_in(key, 11), -4.0, 4.0, (D, HEADS * HEAD_DIM), jnp.float32) * D ** (-0.5)


def draw_w_query(key, part):
    return shared_matrix(key).astype(jnp.bfloat16)


def draw_w_key(key, part):
    fresh = jax.random.truncated_normal(jax.random.fold_in(key, 31), -4.0, 4.0, (D, HEADS * HEAD_DIM), jnp.float32)
    return (fresh * D ** (-0.5)).astype(jnp.bfloat16)


def draw_pixels(key, part):
    shape = (TUBELETS, P_SIZE, PIX)
    return jax.random.truncated_normal(jax.random.fold_in(key, 53), -4.0, 4.0, shape, jnp.float32).astype(jnp.bfloat16)


def gaussian(stream_key, dims, scale, bound, kind=jnp.bfloat16):
    array = scale * jax.random.normal(stream_key, dims, jnp.float32)
    return jnp.clip(array, min=-bound, max=bound).astype(kind)


def setup_inputs(seed: int = 0, part: int = 0) -> dict:
    splits = jax.random.split(jax.random.key(seed), 9)
    part_keys = jax.random.split(jax.random.fold_in(splits[8], part), 9)
    return {
        "pixels": draw_pixels(jax.random.fold_in(jax.random.fold_in(splits[8], part), 71), part),
        "prior_kv": gaussian(part_keys[1], (2, WINDOW, P_SIZE, HEADS * HEAD_DIM), 1.0, 6.0),
        "w_embed": gaussian(splits[2], (PIX, D), PIX ** -0.5, 0.15625),
        "ln_gain": jnp.clip(1.0 + 0.18 * jax.random.normal(splits[3], (D,), jnp.float32), 0.1, 1.9),
        "w_query": draw_w_query(jax.random.fold_in(splits[8], 71), part),
        "w_key": draw_w_key(jax.random.fold_in(splits[8], 71), part),
        "w_value": gaussian(splits[6], (D, HEADS * HEAD_DIM), D ** -0.5, 0.15625),
        "w_out": gaussian(splits[7], (HEADS * HEAD_DIM, D), (HEADS * HEAD_DIM) ** -0.5, 0.25),
    }


def reference(pixels, prior_kv, w_embed, ln_gain, w_query, w_key, w_value, w_out):
    tub, pat, pix = pixels.shape
    flat = pixels.reshape(tub * pat, pix)
    embedded = jnp.dot(flat, w_embed, preferred_element_type=jnp.float32).astype(jnp.bfloat16)
    e_wide = embedded.astype(jnp.float32)
    center = e_wide - lax.optimization_barrier(jnp.mean(e_wide, axis=-1, keepdims=True))
    spread = lax.optimization_barrier(jnp.mean(center * center, axis=-1, keepdims=True))
    normed = (center * lax.rsqrt(spread + 1e-06) * ln_gain).astype(jnp.bfloat16)
    shape4 = (tub, pat, HEADS, HEAD_DIM)
    query = jnp.dot(normed, w_query, preferred_element_type=jnp.float32).astype(jnp.bfloat16).reshape(shape4)
    key = jnp.dot(normed, w_key, preferred_element_type=jnp.float32).astype(jnp.bfloat16).reshape(shape4)
    value = jnp.dot(normed, w_value, preferred_element_type=jnp.float32).astype(jnp.bfloat16).reshape(shape4)
    scale = 1.0 / math.sqrt(HEAD_DIM)
    prior_key = prior_kv[0].reshape(WINDOW, pat, HEADS, HEAD_DIM)
    prior_value = prior_kv[1].reshape(WINDOW, pat, HEADS, HEAD_DIM)
    key_pad = jnp.concatenate([prior_key, key], axis=0)
    value_pad = jnp.concatenate([prior_value, value], axis=0)
    query_wide = query.astype(jnp.float32)
    score_list = []
    for offset in range(WINDOW + 1):
        shifted = key_pad[WINDOW - offset:WINDOW - offset + tub].astype(jnp.float32)
        score_list.append(jnp.einsum('tphe,tphe->thp', query_wide, shifted) * scale)
    scores = jnp.stack(score_list, axis=0)
    top = lax.optimization_barrier(jnp.max(scores, axis=0, keepdims=True))
    expo = jnp.exp(scores - top)
    weights = (expo / lax.optimization_barrier(jnp.sum(expo, axis=0, keepdims=True))).astype(jnp.bfloat16)
    mixed = jnp.zeros((tub, pat, HEADS, HEAD_DIM), jnp.float32)
    for offset in range(WINDOW + 1):
        shifted = value_pad[WINDOW - offset:WINDOW - offset + tub].astype(jnp.float32)
        mixed = mixed + jnp.einsum('thp,tphe->tphe', weights[offset].astype(jnp.float32), shifted)
    mixed = mixed.astype(jnp.bfloat16).reshape(tub * pat, HEADS * HEAD_DIM)
    encoded = e_wide + jnp.dot(mixed, w_out, preferred_element_type=jnp.float32)
    return encoded.astype(jnp.bfloat16).reshape(tub, pat, D)
```

```python
import functools
import math

import jax
import jax.numpy as jnp
from jax import lax
from jax.experimental import pallas as pl
from jax.experimental.pallas import tpu as pltpu
from jax.sharding import PartitionSpec as P

HEADS = 8
HEAD_DIM = 80
LANE = 128
CHUNK = 16
GROUP = 2
MESH = pl.DeviceIdType.MESH


def kernel(
    pixels,
    prior,
    w_embed,
    ln_gain,
    w_query,
    w_key,
    w_value,
    w_out,
    encoded,
    pix,
    we,
    gain,
    wq,
    wk,
    wv,
    wo,
    emb,
    qry,
    kv,
    out,
    mask,
    w_sem,
    pix_sem,
    prior_sem,
    out_sem,
    far_send,
    far_recv,
    near_send,
    near_recv,
):
    count = lax.axis_size("tm")
    me = lax.axis_index("tm")
    tub = pixels.shape[0]
    chunks = pixels.shape[1] // CHUNK
    half = kv.shape[3] // 2
    width = emb.shape[3]
    rows = tub * CHUNK
    is_even = lax.rem(me, 2) == 0
    partner = jnp.where(is_even, me + 1, me - 1)
    has_before = me >= 2
    has_after = me + 2 < count

    barrier = pltpu.get_barrier_semaphore()
    pl.semaphore_signal(barrier, inc=1, device_id={"tm": partner}, device_id_type=MESH)

    @pl.when(has_before)
    def _():
        pl.semaphore_signal(barrier, inc=1, device_id={"tm": me - 2}, device_id_type=MESH)

    @pl.when(has_after)
    def _():
        pl.semaphore_signal(barrier, inc=1, device_id={"tm": me + 2}, device_id_type=MESH)

    def patches(c):
        return pl.ds(pl.multiple_of(c * CHUNK, CHUNK), CHUNK)

    def load_pix(c):
        return pltpu.make_async_copy(pixels.at[:, patches(c), :], pix.at[c], pix_sem.at[c])

    def load_weight(source, target, index):
        return pltpu.make_async_copy(source, target, w_sem.at[index])

    get_we = load_weight(w_embed, we, 0)
    get_gain = load_weight(ln_gain, gain, 1)
    get_wk = load_weight(w_key, wk, 2)
    get_wv = load_weight(w_value, wv, 3)
    get_wq = load_weight(w_query, wq, 4)
    get_wo = load_weight(w_out, wo, 5)

    def load_prior(c, which, first, slot, index):
        return pltpu.make_async_copy(
            prior.at[which, pl.ds(first, tub), patches(c), :],
            kv.at[c, pl.ds(slot, tub), :, pl.ds(which * half, half)],
            prior_sem.at[index, which, c],
        )

    def send_far(c):
        return pltpu.make_async_remote_copy(
            src_ref=kv.at[c, pl.ds(2 * tub, tub)],
            dst_ref=kv.at[c, pl.ds(0, tub)],
            send_sem=far_send.at[c],
            recv_sem=far_recv.at[c],
            device_id={"tm": me + 2},
            device_id_type=MESH,
        )

    def send_near(c, slot):
        return pltpu.make_async_remote_copy(
            src_ref=kv.at[c, pl.ds(slot, tub)],
            dst_ref=kv.at[c, pl.ds(tub, tub)],
            send_sem=near_send.at[c],
            recv_sem=near_recv.at[c],
            device_id={"tm": partner},
            device_id_type=MESH,
        )

    def store_out(c):
        return pltpu.make_async_copy(out.at[c], encoded.at[:, patches(c), :], out_sem.at[c])

    for c in range(GROUP):
        load_pix(c).start()
    get_we.start()
    get_gain.start()
    get_wk.start()
    get_wv.start()
    get_wq.start()
    for c in range(GROUP, chunks):
        load_pix(c).start()
    get_wo.start()

    @pl.when(me == 0)
    def _():
        def start(c, carry):
            for which in range(2):
                load_prior(c, which, 0, 0, 0).start()
                load_prior(c, which, tub, tub, 1).start()
            return carry

        lax.fori_loop(0, chunks, start, 0)

    @pl.when(me == 1)
    def _():
        def start(c, carry):
            for which in range(2):
                load_prior(c, which, tub, 0, 0).start()
            return carry

        lax.fori_loop(0, chunks, start, 0)

    total = 2 * rows
    keys = 3 * tub * CHUNK
    row = lax.broadcasted_iota(jnp.int32, (total, keys), 0)
    col = lax.broadcasted_iota(jnp.int32, (total, keys), 1)
    step_t = lax.rem(row, rows) // CHUNK
    step_s = col // CHUNK
    same = lax.rem(row, CHUNK) == lax.rem(col, CHUNK)
    valid = same & (step_s >= step_t) & (step_s <= step_t + 2 * tub)
    mask[...] = jnp.where(valid, 1.0, 0.0)

    def project(s, carry):
        first = s * GROUP
        for g in range(GROUP):
            load_pix(first + g).wait()

        @pl.when(s == 0)
        def _():
            get_we.wait()
            get_gain.wait()

        flat = pix[pl.ds(first, GROUP)].reshape(GROUP * rows, pix.shape[3])
        embedded = jnp.dot(flat, we[...], preferred_element_type=jnp.float32).astype(jnp.bfloat16)
        emb[pl.ds(first, GROUP)] = embedded.reshape(GROUP, tub, CHUNK, width)
        wide = embedded.astype(jnp.float32)
        center = wide - jnp.mean(wide, axis=-1, keepdims=True)
        spread = jnp.mean(center * center, axis=-1, keepdims=True)
        normed = (center * lax.rsqrt(spread + 1e-06) * gain[...]).astype(jnp.bfloat16)

        @pl.when(s == 0)
        def _():
            get_wk.wait()
            get_wv.wait()

        shape4 = (GROUP, tub, CHUNK, half)
        key = jnp.dot(normed, wk[...], preferred_element_type=jnp.float32).astype(jnp.bfloat16)
        kv[pl.ds(first, GROUP), pl.ds(2 * tub, tub), :, pl.ds(0, half)] = key.reshape(shape4)
        value = jnp.dot(normed, wv[...], preferred_element_type=jnp.float32).astype(jnp.bfloat16)
        kv[pl.ds(first, GROUP), pl.ds(2 * tub, tub), :, pl.ds(half, half)] = value.reshape(shape4)

        @pl.when(s == 0)
        def _():
            expected = 1 + has_before.astype(jnp.int32) + has_after.astype(jnp.int32)
            pl.semaphore_wait(barrier, expected)

        for g in range(GROUP):

            @pl.when(has_after)
            def _():
                send_far(first + g).start()

            @pl.when(is_even)
            def _():
                send_near(first + g, 2 * tub).start()

        @pl.when(s == 0)
        def _():
            get_wq.wait()

        query = jnp.dot(normed, wq[...], preferred_element_type=jnp.float32).astype(jnp.bfloat16)
        qry[pl.ds(first, GROUP)] = query.reshape(shape4)
        return carry

    lax.fori_loop(0, chunks // GROUP, project, 0)
    get_wo.wait()

    @pl.when(me == 0)
    def _():
        def finish(c, carry):
            for which in range(2):
                load_prior(c, which, 0, 0, 0).wait()
                load_prior(c, which, tub, tub, 1).wait()
            return carry

        lax.fori_loop(0, chunks, finish, 0)

    @pl.when(me == 1)
    def _():
        def finish(c, carry):
            for which in range(2):
                load_prior(c, which, tub, 0, 0).wait()
            return carry

        lax.fori_loop(0, chunks, finish, 0)

    scale = 1.0 / math.sqrt(HEAD_DIM)
    window = 2 * LANE
    lane = lax.broadcasted_iota(jnp.int32, (1, window), 1)

    def attend(c, carry):
        @pl.when(has_before)
        def _():
            send_far(c).wait_recv()

        @pl.when(has_before & jnp.logical_not(is_even))
        def _():
            send_near(c, 0).start()

        @pl.when(has_before | jnp.logical_not(is_even))
        def _():
            send_near(c, 0).wait_recv()

        tiles = [None] * (half // LANE)
        for pair in range(HEADS // 2):
            low = 2 * pair * HEAD_DIM
            base = low // LANE * LANE
            picks = []
            for head in range(2):
                begin = low + head * HEAD_DIM - base
                picks.append(jnp.where((lane >= begin) & (lane < begin + HEAD_DIM), 1.0, 0.0))
            q = qry[c, :, :, pl.ds(base, window)].reshape(rows, window)
            both = jnp.concatenate([q * pick.astype(jnp.bfloat16) for pick in picks], axis=0)
            k = kv[c, :, :, pl.ds(base, window)].reshape(keys, window)
            scores = lax.dot_general(
                both, k, (((1,), (1,)), ((), ())), preferred_element_type=jnp.float32
            )
            scores = jnp.where(mask[...] > 0.5, scores * scale, -jnp.inf)
            top = jnp.max(scores, axis=-1, keepdims=True)
            expo = jnp.exp(scores - top)
            weights = (expo / jnp.sum(expo, axis=-1, keepdims=True)).astype(jnp.bfloat16)
            v = kv[c, :, :, pl.ds(half + base, window)].reshape(keys, window)
            mixed = jnp.dot(weights, v, preferred_element_type=jnp.float32)
            part = mixed[:rows] * picks[0] + mixed[rows:] * picks[1]
            for side in range(2):
                piece = part[:, side * LANE : (side + 1) * LANE]
                at = base // LANE + side
                tiles[at] = piece if tiles[at] is None else tiles[at] + piece
        mixed = jnp.concatenate(tiles, axis=1).astype(jnp.bfloat16)
        result = emb[c].reshape(rows, width).astype(jnp.float32) + jnp.dot(
            mixed, wo[...], preferred_element_type=jnp.float32
        )
        out[c] = result.astype(jnp.bfloat16).reshape(tub, CHUNK, width)
        store_out(c).start()
        return carry

    lax.fori_loop(0, chunks, attend, 0)

    def drain(c, carry):
        store_out(c).wait()

        @pl.when(has_after)
        def _():
            send_far(c).wait_send()

        @pl.when(has_before | is_even)
        def _():
            send_near(c, 0).wait_send()

        return carry

    lax.fori_loop(0, chunks, drain, 0)


def body(pixels, prior_kv, w_embed, ln_gain, w_query, w_key, w_value, w_out):
    tub, pat, pix = pixels.shape
    width = w_embed.shape[1]
    half = w_key.shape[1]
    chunks = pat // CHUNK
    bf16 = jnp.bfloat16
    dma = pltpu.SemaphoreType.DMA
    return pl.pallas_call(
        kernel,
        out_shape=jax.ShapeDtypeStruct((tub, pat, width), bf16),
        in_specs=[pl.BlockSpec(memory_space=pl.ANY)] * 8,
        out_specs=pl.BlockSpec(memory_space=pl.ANY),
        scratch_shapes=[
            pltpu.VMEM((chunks, tub, CHUNK, pix), bf16),
            pltpu.VMEM(w_embed.shape, bf16),
            pltpu.VMEM((1, width), jnp.float32),
            pltpu.VMEM(w_query.shape, bf16),
            pltpu.VMEM(w_key.shape, bf16),
            pltpu.VMEM(w_value.shape, bf16),
            pltpu.VMEM(w_out.shape, bf16),
            pltpu.VMEM((chunks, tub, CHUNK, width), bf16),
            pltpu.VMEM((chunks, tub, CHUNK, half), bf16),
            pltpu.VMEM((chunks, 3 * tub, CHUNK, 2 * half), bf16),
            pltpu.VMEM((chunks, tub, CHUNK, width), bf16),
            pltpu.VMEM((2 * tub * CHUNK, 3 * tub * CHUNK), jnp.float32),
            dma((6,)),
            dma((chunks,)),
            dma((2, 2, chunks)),
            dma((chunks,)),
            dma((chunks,)),
            dma((chunks,)),
            dma((chunks,)),
            dma((chunks,)),
        ],
        compiler_params=pltpu.CompilerParams(collective_id=0, has_side_effects=True),
    )(pixels, prior_kv, w_embed, ln_gain.reshape(1, width), w_query, w_key, w_value, w_out)


def solution(mesh):
    placed = (
        P(("groups", "tm"), None, None),
        P(None, "groups", None, None),
        P(),
        P(),
        P(),
        P(),
        P(),
        P(),
    )
    return jax.shard_map(
        body, mesh=mesh, in_specs=placed, out_specs=P(("groups", "tm"), None, None), check_vma=False
    )
```

```python
import functools
import math

import jax
import jax.numpy as jnp
from jax import lax
from jax.experimental import pallas as pl
from jax.experimental.pallas import tpu as pltpu
from jax.sharding import PartitionSpec as P

HEADS = 8
HEAD_DIM = 80
LANE = 128
CHUNK = 16
GROUP = 2
MESH = pl.DeviceIdType.MESH


def kernel(
    pixels,
    prior,
    w_embed,
    ln_gain,
    w_query,
    w_key,
    w_value,
    w_out,
    encoded,
    pix,
    far_pix,
    we,
    gain,
    wq,
    wk,
    wv,
    wo,
    emb,
    qry,
    kv,
    out,
    mask,
    w_sem,
    pix_sem,
    prior_sem,
    out_sem,
    far_send,
    far_recv,
    near_send,
    near_recv,
    raw_send,
    raw_recv,
):
    count = lax.axis_size("tm")
    me = lax.axis_index("tm")
    tub = pixels.shape[0]
    chunks = pixels.shape[1] // CHUNK
    half = kv.shape[3] // 2
    width = emb.shape[3]
    rows = tub * CHUNK
    is_even = lax.rem(me, 2) == 0
    is_odd = jnp.logical_not(is_even)
    partner = jnp.where(is_even, me + 1, me - 1)
    has_before = me >= 2
    steps = chunks // GROUP
    turn = lax.rem(me, 2)
    has_after = me + 2 < count

    barrier = pltpu.get_barrier_semaphore()
    pl.semaphore_signal(barrier, inc=1, device_id={"tm": partner}, device_id_type=MESH)

    @pl.when(has_before)
    def _():
        pl.semaphore_signal(barrier, inc=1, device_id={"tm": me - 2}, device_id_type=MESH)

    @pl.when(has_after)
    def _():
        pl.semaphore_signal(barrier, inc=1, device_id={"tm": me + 2}, device_id_type=MESH)

    def patches(c):
        return pl.ds(pl.multiple_of(c * CHUNK, CHUNK), CHUNK)

    def load_pix(c):
        return pltpu.make_async_copy(pixels.at[:, patches(c), :], pix.at[c], pix_sem.at[c])

    def load_weight(source, target, index):
        return pltpu.make_async_copy(source, target, w_sem.at[index])

    get_we = load_weight(w_embed, we, 0)
    get_gain = load_weight(ln_gain, gain, 1)
    get_wk = load_weight(w_key, wk, 2)
    get_wv = load_weight(w_value, wv, 3)
    get_wq = load_weight(w_query, wq, 4)
    get_wo = load_weight(w_out, wo, 5)

    def load_prior(c, which, first, slot, index):
        return pltpu.make_async_copy(
            prior.at[which, pl.ds(first, tub), patches(c), :],
            kv.at[c, pl.ds(slot, tub), :, pl.ds(which * half, half)],
            prior_sem.at[index, which, c],
        )

    def send_far(c):
        return pltpu.make_async_remote_copy(
            src_ref=kv.at[c, pl.ds(2 * tub, tub)],
            dst_ref=kv.at[c, pl.ds(0, tub)],
            send_sem=far_send.at[c],
            recv_sem=far_recv.at[c],
            device_id={"tm": me + 2},
            device_id_type=MESH,
        )

    def send_raw(g):
        return pltpu.make_async_remote_copy(
            src_ref=pixels.at[:, patches(g), :],
            dst_ref=far_pix.at[g],
            send_sem=raw_send.at[g],
            recv_sem=raw_recv.at[g],
            device_id={"tm": me + 2},
            device_id_type=MESH,
        )

    def send_near(c, slot):
        return pltpu.make_async_remote_copy(
            src_ref=kv.at[c, pl.ds(slot, tub)],
            dst_ref=kv.at[c, pl.ds(tub, tub)],
            send_sem=near_send.at[c],
            recv_sem=near_recv.at[c],
            device_id={"tm": partner},
            device_id_type=MESH,
        )

    def store_out(c):
        return pltpu.make_async_copy(out.at[c], encoded.at[:, patches(c), :], out_sem.at[c])

    for g in range(GROUP):
        load_pix(lax.rem(turn, steps) * GROUP + g).start()
    get_we.start()
    get_gain.start()
    get_wk.start()
    get_wv.start()
    get_wq.start()
    for s in range(1, steps):
        for g in range(GROUP):
            load_pix(lax.rem(s + turn, steps) * GROUP + g).start()
    get_wo.start()

    @pl.when(me == 0)
    def _():
        def start(c, carry):
            for which in range(2):
                load_prior(c, which, 0, 0, 0).start()
                load_prior(c, which, tub, tub, 1).start()
            return carry

        lax.fori_loop(0, chunks, start, 0)

    @pl.when(me == 1)
    def _():
        def start(c, carry):
            for which in range(2):
                load_prior(c, which, tub, 0, 0).start()
            return carry

        lax.fori_loop(0, chunks, start, 0)

    expected = 1 + has_before.astype(jnp.int32) + has_after.astype(jnp.int32)
    pl.semaphore_wait(barrier, expected)

    @pl.when(has_after & is_odd)
    def _():
        for g in range(GROUP):
            send_raw(g).start()

    total = 2 * rows
    keys = 3 * tub * CHUNK
    row = lax.broadcasted_iota(jnp.int32, (total, keys), 0)
    col = lax.broadcasted_iota(jnp.int32, (total, keys), 1)
    step_t = lax.rem(row, rows) // CHUNK
    step_s = col // CHUNK
    same = lax.rem(row, CHUNK) == lax.rem(col, CHUNK)
    valid = same & (step_s >= step_t) & (step_s <= step_t + 2 * tub)
    mask[...] = jnp.where(valid, 1.0, 0.0)


    def normalize(flat):
        embedded = jnp.dot(flat, we[...], preferred_element_type=jnp.float32).astype(jnp.bfloat16)
        wide = embedded.astype(jnp.float32)
        center = wide - jnp.mean(wide, axis=-1, keepdims=True)
        spread = jnp.mean(center * center, axis=-1, keepdims=True)
        scaled = center * lax.rsqrt(spread + 1e-06) * gain[...].reshape(1, width)
        return embedded, scaled.astype(jnp.bfloat16)

    shape4 = (GROUP, tub, CHUNK, half)

    def fill(normed, first, slot):
        for weight, lane in ((wk, 0), (wv, half)):
            part = jnp.dot(normed, weight[...], preferred_element_type=jnp.float32)
            kv[pl.ds(first, GROUP), pl.ds(slot, tub), :, pl.ds(lane, half)] = part.astype(
                jnp.bfloat16
            ).reshape(shape4)

    def project(s, carry):
        first = lax.rem(s + turn, steps) * GROUP
        for g in range(GROUP):
            load_pix(first + g).wait()

        @pl.when(s == 0)
        def _():
            get_we.wait()
            get_gain.wait()

        flat = pix[pl.ds(first, GROUP)].reshape(GROUP * rows, pix.shape[3])
        embedded, normed = normalize(flat)
        emb[pl.ds(first, GROUP)] = embedded.reshape(GROUP, tub, CHUNK, width)

        @pl.when(s == 0)
        def _():
            get_wk.wait()
            get_wv.wait()

        fill(normed, first, 2 * tub)

        for g in range(GROUP):

            @pl.when(has_after & (is_even | (first > 0)))
            def _():
                send_far(first + g).start()

            @pl.when(is_even)
            def _():
                send_near(first + g, 2 * tub).start()

        @pl.when(s == 0)
        def _():
            get_wq.wait()

        query = jnp.dot(normed, wq[...], preferred_element_type=jnp.float32).astype(jnp.bfloat16)
        qry[pl.ds(first, GROUP)] = query.reshape(shape4)
        return carry

    lax.fori_loop(0, steps, project, 0)

    @pl.when(has_before & is_odd)
    def _():
        for g in range(GROUP):
            send_raw(g).wait_recv()
        _, normed = normalize(far_pix[...].reshape(GROUP * rows, pix.shape[3]))
        fill(normed, 0, 0)

    get_wo.wait()

    @pl.when(me == 0)
    def _():
        def finish(c, carry):
            for which in range(2):
                load_prior(c, which, 0, 0, 0).wait()
                load_prior(c, which, tub, tub, 1).wait()
            return carry

        lax.fori_loop(0, chunks, finish, 0)

    @pl.when(me == 1)
    def _():
        def finish(c, carry):
            for which in range(2):
                load_prior(c, which, tub, 0, 0).wait()
            return carry

        lax.fori_loop(0, chunks, finish, 0)

    scale = 1.0 / math.sqrt(HEAD_DIM)
    window = 2 * LANE
    lane = lax.broadcasted_iota(jnp.int32, (1, window), 1)

    def attend(c, carry):
        @pl.when(has_before & (is_even | (c >= GROUP)))
        def _():
            send_far(c).wait_recv()

        @pl.when(has_before & is_odd)
        def _():
            send_near(c, 0).start()

        @pl.when(has_before | is_odd)
        def _():
            send_near(c, 0).wait_recv()

        tiles = [None] * (half // LANE)
        for pair in range(HEADS // 2):
            low = 2 * pair * HEAD_DIM
            base = low // LANE * LANE
            picks = []
            for head in range(2):
                begin = low + head * HEAD_DIM - base
                picks.append(jnp.where((lane >= begin) & (lane < begin + HEAD_DIM), 1.0, 0.0))
            q = qry[c, :, :, pl.ds(base, window)].reshape(rows, window)
            both = jnp.concatenate([q * pick.astype(jnp.bfloat16) for pick in picks], axis=0)
            k = kv[c, :, :, pl.ds(base, window)].reshape(keys, window)
            scores = lax.dot_general(
                both, k, (((1,), (1,)), ((), ())), preferred_element_type=jnp.float32
            )
            scores = jnp.where(mask[...] > 0.5, scores * scale, -jnp.inf)
            top = jnp.max(scores, axis=-1, keepdims=True)
            expo = jnp.exp(scores - top)
            weights = (expo / jnp.sum(expo, axis=-1, keepdims=True)).astype(jnp.bfloat16)
            v = kv[c, :, :, pl.ds(half + base, window)].reshape(keys, window)
            mixed = jnp.dot(weights, v, preferred_element_type=jnp.float32)
            part = mixed[:rows] * picks[0] + mixed[rows:] * picks[1]
            for side in range(2):
                piece = part[:, side * LANE : (side + 1) * LANE]
                at = base // LANE + side
                tiles[at] = piece if tiles[at] is None else tiles[at] + piece
        mixed = jnp.concatenate(tiles, axis=1).astype(jnp.bfloat16)
        result = emb[c].reshape(rows, width).astype(jnp.float32) + jnp.dot(
            mixed, wo[...], preferred_element_type=jnp.float32
        )
        out[c] = result.astype(jnp.bfloat16).reshape(tub, CHUNK, width)
        store_out(c).start()
        return carry

    lax.fori_loop(0, chunks, attend, 0)

    def drain(c, carry):
        store_out(c).wait()

        @pl.when(has_after & (is_even | (c >= GROUP)))
        def _():
            send_far(c).wait_send()

        @pl.when(has_before | is_even)
        def _():
            send_near(c, 0).wait_send()

        return carry

    lax.fori_loop(0, chunks, drain, 0)

    @pl.when(has_after & is_odd)
    def _():
        for g in range(GROUP):
            send_raw(g).wait_send()


def body(pixels, prior_kv, w_embed, ln_gain, w_query, w_key, w_value, w_out):
    tub, pat, pix = pixels.shape
    width = w_embed.shape[1]
    half = w_key.shape[1]
    chunks = pat // CHUNK
    bf16 = jnp.bfloat16
    dma = pltpu.SemaphoreType.DMA
    return pl.pallas_call(
        kernel,
        out_shape=jax.ShapeDtypeStruct((tub, pat, width), bf16),
        in_specs=[pl.BlockSpec(memory_space=pl.ANY)] * 8,
        out_specs=pl.BlockSpec(memory_space=pl.ANY),
        scratch_shapes=[
            pltpu.VMEM((chunks, tub, CHUNK, pix), bf16),
            pltpu.VMEM((GROUP, tub, CHUNK, pix), bf16),
            pltpu.VMEM(w_embed.shape, bf16),
            pltpu.VMEM((width,), jnp.float32),
            pltpu.VMEM(w_query.shape, bf16),
            pltpu.VMEM(w_key.shape, bf16),
            pltpu.VMEM(w_value.shape, bf16),
            pltpu.VMEM(w_out.shape, bf16),
            pltpu.VMEM((chunks, tub, CHUNK, width), bf16),
            pltpu.VMEM((chunks, tub, CHUNK, half), bf16),
            pltpu.VMEM((chunks, 3 * tub, CHUNK, 2 * half), bf16),
            pltpu.VMEM((chunks, tub, CHUNK, width), bf16),
            pltpu.VMEM((2 * tub * CHUNK, 3 * tub * CHUNK), jnp.float32),
            dma((6,)),
            dma((chunks,)),
            dma((2, 2, chunks)),
            dma((chunks,)),
            dma((chunks,)),
            dma((chunks,)),
            dma((chunks,)),
            dma((chunks,)),
            dma((GROUP,)),
            dma((GROUP,)),
        ],
        compiler_params=pltpu.CompilerParams(collective_id=0, has_side_effects=True),
    )(pixels, prior_kv, w_embed, ln_gain, w_query, w_key, w_value, w_out)


def solution(mesh):
    placed = (
        P(("groups", "tm"), None, None),
        P(None, "groups", None, None),
        P(),
        P(),
        P(),
        P(),
        P(),
        P(),
    )
    return jax.shard_map(
        body, mesh=mesh, in_specs=placed, out_specs=P(("groups", "tm"), None, None), check_vma=False
    )
```

```python
import functools
import math

import jax
import jax.numpy as jnp
from jax import lax
from jax.experimental import pallas as pl
from jax.experimental.pallas import tpu as pltpu
from jax.sharding import PartitionSpec as P

HEADS = 8
HEAD_DIM = 80
LANE = 128
CHUNK = 16
GROUP = 2
MESH = pl.DeviceIdType.MESH


def kernel(
    pixels,
    prior,
    w_embed,
    ln_gain,
    w_query,
    w_key,
    w_value,
    w_out,
    encoded,
    pix,
    far_pix,
    we,
    gain,
    wq,
    wk,
    wv,
    wo,
    emb,
    qry,
    kv,
    mask,
    w_sem,
    pix_sem,
    prior_sem,
    far_send,
    far_recv,
    near_send,
    near_recv,
    raw_send,
    raw_recv,
):
    count = lax.axis_size("tm")
    me = lax.axis_index("tm")
    tub = pixels.shape[0]
    chunks = pixels.shape[1] // CHUNK
    half = kv.shape[3] // 2
    width = emb.shape[3]
    rows = tub * CHUNK
    is_even = lax.rem(me, 2) == 0
    is_odd = jnp.logical_not(is_even)
    partner = jnp.where(is_even, me + 1, me - 1)
    has_before = me >= 2
    steps = chunks // GROUP
    turn = lax.rem(me, 2)
    has_after = me + 2 < count

    barrier = pltpu.get_barrier_semaphore()
    pl.semaphore_signal(barrier, inc=1, device_id={"tm": partner}, device_id_type=MESH)

    @pl.when(has_before)
    def _():
        pl.semaphore_signal(barrier, inc=1, device_id={"tm": me - 2}, device_id_type=MESH)

    @pl.when(has_after)
    def _():
        pl.semaphore_signal(barrier, inc=1, device_id={"tm": me + 2}, device_id_type=MESH)

    def patches(c):
        return pl.ds(pl.multiple_of(c * CHUNK, CHUNK), CHUNK)

    def load_pix(c):
        return pltpu.make_async_copy(pixels.at[:, patches(c), :], pix.at[c], pix_sem.at[c])

    def load_weight(source, target, index):
        return pltpu.make_async_copy(source, target, w_sem.at[index])

    get_we = load_weight(w_embed, we, 0)
    get_gain = load_weight(ln_gain, gain, 1)
    get_wk = load_weight(w_key, wk, 2)
    get_wv = load_weight(w_value, wv, 3)
    get_wq = load_weight(w_query, wq, 4)
    get_wo = load_weight(w_out, wo, 5)

    def load_prior(c, which, first, slot, index):
        return pltpu.make_async_copy(
            prior.at[which, pl.ds(first, tub), patches(c), :],
            kv.at[c, pl.ds(slot, tub), :, pl.ds(which * half, half)],
            prior_sem.at[index, which, c],
        )

    def send_far(c):
        return pltpu.make_async_remote_copy(
            src_ref=kv.at[c, pl.ds(2 * tub, tub)],
            dst_ref=kv.at[c, pl.ds(0, tub)],
            send_sem=far_send.at[c],
            recv_sem=far_recv.at[c],
            device_id={"tm": me + 2},
            device_id_type=MESH,
        )

    def send_raw(g):
        return pltpu.make_async_remote_copy(
            src_ref=pixels.at[:, patches(g), :],
            dst_ref=far_pix.at[g],
            send_sem=raw_send.at[g],
            recv_sem=raw_recv.at[g],
            device_id={"tm": me + 2},
            device_id_type=MESH,
        )

    def send_near(c, slot):
        return pltpu.make_async_remote_copy(
            src_ref=kv.at[c, pl.ds(slot, tub)],
            dst_ref=kv.at[c, pl.ds(tub, tub)],
            send_sem=near_send.at[c],
            recv_sem=near_recv.at[c],
            device_id={"tm": partner},
            device_id_type=MESH,
        )

    for g in range(GROUP):
        load_pix(lax.rem(turn, steps) * GROUP + g).start()
    get_we.start()
    get_gain.start()
    get_wk.start()
    get_wv.start()
    get_wq.start()
    for s in range(1, steps):
        for g in range(GROUP):
            load_pix(lax.rem(s + turn, steps) * GROUP + g).start()
    get_wo.start()

    @pl.when(me == 0)
    def _():
        def start(c, carry):
            for which in range(2):
                load_prior(c, which, 0, 0, 0).start()
                load_prior(c, which, tub, tub, 1).start()
            return carry

        lax.fori_loop(0, chunks, start, 0)

    @pl.when(me == 1)
    def _():
        def start(c, carry):
            for which in range(2):
                load_prior(c, which, tub, 0, 0).start()
            return carry

        lax.fori_loop(0, chunks, start, 0)

    expected = 1 + has_before.astype(jnp.int32) + has_after.astype(jnp.int32)
    pl.semaphore_wait(barrier, expected)

    @pl.when(has_after & is_odd)
    def _():
        for g in range(GROUP):
            send_raw(g).start()

    total = 2 * rows
    keys = 3 * tub * CHUNK
    row = lax.broadcasted_iota(jnp.int32, (total, keys), 0)
    col = lax.broadcasted_iota(jnp.int32, (total, keys), 1)
    step_t = lax.rem(row, rows) // CHUNK
    step_s = col // CHUNK
    same = lax.rem(row, CHUNK) == lax.rem(col, CHUNK)
    valid = same & (step_s >= step_t) & (step_s <= step_t + 2 * tub)
    mask[...] = jnp.where(valid, 1.0, 0.0)


    def normalize(flat):
        embedded = jnp.dot(flat, we[...], preferred_element_type=jnp.float32).astype(jnp.bfloat16)
        wide = embedded.astype(jnp.float32)
        center = wide - jnp.mean(wide, axis=-1, keepdims=True)
        spread = jnp.mean(center * center, axis=-1, keepdims=True)
        scaled = center * lax.rsqrt(spread + 1e-06) * gain[...].reshape(1, width)
        return embedded, scaled.astype(jnp.bfloat16)

    shape4 = (GROUP, tub, CHUNK, half)

    def fill(normed, first, slot):
        for weight, lane in ((wk, 0), (wv, half)):
            part = jnp.dot(normed, weight[...], preferred_element_type=jnp.float32)
            kv[pl.ds(first, GROUP), pl.ds(slot, tub), :, pl.ds(lane, half)] = part.astype(
                jnp.bfloat16
            ).reshape(shape4)

    def project(s, carry):
        first = lax.rem(s + turn, steps) * GROUP
        for g in range(GROUP):
            load_pix(first + g).wait()

        @pl.when(s == 0)
        def _():
            get_we.wait()
            get_gain.wait()

        flat = pix[pl.ds(first, GROUP)].reshape(GROUP * rows, pix.shape[3])
        embedded, normed = normalize(flat)
        emb[pl.ds(first, GROUP)] = embedded.reshape(GROUP, tub, CHUNK, width)

        @pl.when(s == 0)
        def _():
            get_wk.wait()
            get_wv.wait()

        fill(normed, first, 2 * tub)

        for g in range(GROUP):

            @pl.when(has_after & (is_even | (first > 0)))
            def _():
                send_far(first + g).start()

            @pl.when(is_even)
            def _():
                send_near(first + g, 2 * tub).start()

        @pl.when(s == 0)
        def _():
            get_wq.wait()

        query = jnp.dot(normed, wq[...], preferred_element_type=jnp.float32).astype(jnp.bfloat16)
        qry[pl.ds(first, GROUP)] = query.reshape(shape4)
        return carry

    lax.fori_loop(0, steps, project, 0)

    @pl.when(has_before & is_odd)
    def _():
        for g in range(GROUP):
            send_raw(g).wait_recv()
        _, normed = normalize(far_pix[...].reshape(GROUP * rows, pix.shape[3]))
        fill(normed, 0, 0)

    get_wo.wait()

    @pl.when(me == 0)
    def _():
        def finish(c, carry):
            for which in range(2):
                load_prior(c, which, 0, 0, 0).wait()
                load_prior(c, which, tub, tub, 1).wait()
            return carry

        lax.fori_loop(0, chunks, finish, 0)

    @pl.when(me == 1)
    def _():
        def finish(c, carry):
            for which in range(2):
                load_prior(c, which, tub, 0, 0).wait()
            return carry

        lax.fori_loop(0, chunks, finish, 0)

    scale = 1.0 / math.sqrt(HEAD_DIM)
    window = 2 * LANE
    lane = lax.broadcasted_iota(jnp.int32, (1, window), 1)

    def attend(c, carry):
        @pl.when(has_before & (is_even | (c >= GROUP)))
        def _():
            send_far(c).wait_recv()

        @pl.when(has_before & is_odd)
        def _():
            send_near(c, 0).start()

        @pl.when(has_before | is_odd)
        def _():
            send_near(c, 0).wait_recv()

        tiles = [None] * (half // LANE)
        for pair in range(HEADS // 2):
            low = 2 * pair * HEAD_DIM
            base = low // LANE * LANE
            picks = []
            for head in range(2):
                begin = low + head * HEAD_DIM - base
                picks.append(jnp.where((lane >= begin) & (lane < begin + HEAD_DIM), 1.0, 0.0))
            q = qry[c, :, :, pl.ds(base, window)].reshape(rows, window)
            both = jnp.concatenate([q * pick.astype(jnp.bfloat16) for pick in picks], axis=0)
            k = kv[c, :, :, pl.ds(base, window)].reshape(keys, window)
            scores = lax.dot_general(
                both, k, (((1,), (1,)), ((), ())), preferred_element_type=jnp.float32
            )
            scores = jnp.where(mask[...] > 0.5, scores * scale, -jnp.inf)
            top = jnp.max(scores, axis=-1, keepdims=True)
            expo = jnp.exp(scores - top)
            weights = (expo / jnp.sum(expo, axis=-1, keepdims=True)).astype(jnp.bfloat16)
            v = kv[c, :, :, pl.ds(half + base, window)].reshape(keys, window)
            mixed = jnp.dot(weights, v, preferred_element_type=jnp.float32)
            part = mixed[:rows] * picks[0] + mixed[rows:] * picks[1]
            for side in range(2):
                piece = part[:, side * LANE : (side + 1) * LANE]
                at = base // LANE + side
                tiles[at] = piece if tiles[at] is None else tiles[at] + piece
        mixed = jnp.concatenate(tiles, axis=1).astype(jnp.bfloat16)
        result = emb[c].reshape(rows, width).astype(jnp.float32) + jnp.dot(
            mixed, wo[...], preferred_element_type=jnp.float32
        )
        encoded[:, patches(c), :] = result.astype(jnp.bfloat16).reshape(tub, CHUNK, width)
        return carry

    lax.fori_loop(0, chunks, attend, 0)

    def drain(c, carry):
        @pl.when(has_after & (is_even | (c >= GROUP)))
        def _():
            send_far(c).wait_send()

        @pl.when(has_before | is_even)
        def _():
            send_near(c, 0).wait_send()

        return carry

    lax.fori_loop(0, chunks, drain, 0)

    @pl.when(has_after & is_odd)
    def _():
        for g in range(GROUP):
            send_raw(g).wait_send()


def body(pixels, prior_kv, w_embed, ln_gain, w_query, w_key, w_value, w_out):
    tub, pat, pix = pixels.shape
    width = w_embed.shape[1]
    half = w_key.shape[1]
    chunks = pat // CHUNK
    bf16 = jnp.bfloat16
    dma = pltpu.SemaphoreType.DMA
    return pl.pallas_call(
        kernel,
        out_shape=pltpu.VMEM((tub, pat, width), bf16),
        in_specs=[pl.BlockSpec(memory_space=pl.ANY)] * 8,
        out_specs=pl.BlockSpec(memory_space=pltpu.VMEM),
        scratch_shapes=[
            pltpu.VMEM((chunks, tub, CHUNK, pix), bf16),
            pltpu.VMEM((GROUP, tub, CHUNK, pix), bf16),
            pltpu.VMEM(w_embed.shape, bf16),
            pltpu.VMEM((width,), jnp.float32),
            pltpu.VMEM(w_query.shape, bf16),
            pltpu.VMEM(w_key.shape, bf16),
            pltpu.VMEM(w_value.shape, bf16),
            pltpu.VMEM(w_out.shape, bf16),
            pltpu.VMEM((chunks, tub, CHUNK, width), bf16),
            pltpu.VMEM((chunks, tub, CHUNK, half), bf16),
            pltpu.VMEM((chunks, 3 * tub, CHUNK, 2 * half), bf16),
            pltpu.VMEM((2 * tub * CHUNK, 3 * tub * CHUNK), jnp.float32),
            dma((6,)),
            dma((chunks,)),
            dma((2, 2, chunks)),
            dma((chunks,)),
            dma((chunks,)),
            dma((chunks,)),
            dma((chunks,)),
            dma((GROUP,)),
            dma((GROUP,)),
        ],
        compiler_params=pltpu.CompilerParams(collective_id=0, has_side_effects=True, vmem_limit_bytes=65500000),
    )(pixels, prior_kv, w_embed, ln_gain, w_query, w_key, w_value, w_out)


def solution(mesh):
    placed = (
        P(("groups", "tm"), None, None),
        P(None, "groups", None, None),
        P(),
        P(),
        P(),
        P(),
        P(),
        P(),
    )
    return jax.shard_map(
        body, mesh=mesh, in_specs=placed, out_specs=P(("groups", "tm"), None, None), check_vma=False
    )
```

```python
import functools
import math

import jax
import jax.numpy as jnp
from jax import lax
from jax.experimental import pallas as pl
from jax.experimental.pallas import tpu as pltpu
from jax.sharding import PartitionSpec as P

HEADS = 8
HEAD_DIM = 80
LANE = 128
CHUNK = 16
GROUP = 2
MESH = pl.DeviceIdType.MESH


def kernel(
    pixels,
    prior,
    w_embed,
    ln_gain,
    w_query,
    w_key,
    w_value,
    w_out,
    encoded,
    pix,
    far_pix,
    we,
    gain,
    wq,
    wk,
    wv,
    wo,
    emb,
    qry,
    kv,
    mask,
    w_sem,
    pix_sem,
    prior_sem,
    far_send,
    far_recv,
    near_send,
    near_recv,
    raw_send,
    raw_recv,
):
    count = lax.axis_size("tm")
    me = lax.axis_index("tm")
    tub = pixels.shape[0]
    chunks = pixels.shape[1] // CHUNK
    half = kv.shape[3] // 2
    width = emb.shape[3]
    rows = tub * CHUNK
    near, own, far = 0, tub, 2 * tub
    is_even = lax.rem(me, 2) == 0
    is_odd = jnp.logical_not(is_even)
    partner = jnp.where(is_even, me + 1, me - 1)
    has_before = me >= 2
    steps = chunks // GROUP
    turn = lax.rem(me, 2)
    has_after = me + 2 < count

    barrier = pltpu.get_barrier_semaphore()
    pl.semaphore_signal(barrier, inc=1, device_id={"tm": partner}, device_id_type=MESH)

    @pl.when(has_before)
    def _():
        pl.semaphore_signal(barrier, inc=1, device_id={"tm": me - 2}, device_id_type=MESH)

    @pl.when(has_after)
    def _():
        pl.semaphore_signal(barrier, inc=1, device_id={"tm": me + 2}, device_id_type=MESH)

    def patches(c):
        return pl.ds(pl.multiple_of(c * CHUNK, CHUNK), CHUNK)

    def load_pix(c):
        return pltpu.make_async_copy(pixels.at[:, patches(c), :], pix.at[c], pix_sem.at[c])

    def load_weight(source, target, index):
        return pltpu.make_async_copy(source, target, w_sem.at[index])

    get_we = load_weight(w_embed, we, 0)
    get_gain = load_weight(ln_gain, gain, 1)
    get_wk = load_weight(w_key, wk, 2)
    get_wv = load_weight(w_value, wv, 3)
    get_wq = load_weight(w_query, wq, 4)
    get_wo = load_weight(w_out, wo, 5)

    def load_prior(c, which, first, slot, index):
        return pltpu.make_async_copy(
            prior.at[which, pl.ds(first, tub), patches(c), :],
            kv.at[c, pl.ds(slot, tub), :, pl.ds(which * half, half)],
            prior_sem.at[index, which, c],
        )

    def send_far(c, which):
        lanes = pl.ds(which * half, half)
        return pltpu.make_async_remote_copy(
            src_ref=kv.at[c, pl.ds(own, tub), :, lanes],
            dst_ref=kv.at[c, pl.ds(far, tub), :, lanes],
            send_sem=far_send.at[which, c],
            recv_sem=far_recv.at[which, c],
            device_id={"tm": me + 2},
            device_id_type=MESH,
        )

    def send_raw(g):
        return pltpu.make_async_remote_copy(
            src_ref=pixels.at[:, patches(g), :],
            dst_ref=far_pix.at[g],
            send_sem=raw_send.at[g],
            recv_sem=raw_recv.at[g],
            device_id={"tm": me + 2},
            device_id_type=MESH,
        )

    def send_near(c, slot):
        return pltpu.make_async_remote_copy(
            src_ref=kv.at[c, pl.ds(slot, tub)],
            dst_ref=kv.at[c, pl.ds(near, tub)],
            send_sem=near_send.at[c],
            recv_sem=near_recv.at[c],
            device_id={"tm": partner},
            device_id_type=MESH,
        )

    for g in range(GROUP):
        load_pix(lax.rem(turn, steps) * GROUP + g).start()
    get_we.start()
    get_gain.start()
    get_wk.start()
    get_wv.start()
    get_wq.start()
    for s in range(1, steps):
        for g in range(GROUP):
            load_pix(lax.rem(s + turn, steps) * GROUP + g).start()
    get_wo.start()

    @pl.when(me == 0)
    def _():
        def start(c, carry):
            for which in range(2):
                load_prior(c, which, 0, far, 0).start()
                load_prior(c, which, tub, near, 1).start()
            return carry

        lax.fori_loop(0, chunks, start, 0)

    @pl.when(me == 1)
    def _():
        def start(c, carry):
            for which in range(2):
                load_prior(c, which, tub, far, 0).start()
            return carry

        lax.fori_loop(0, chunks, start, 0)

    expected = 1 + has_before.astype(jnp.int32) + has_after.astype(jnp.int32)
    pl.semaphore_wait(barrier, expected)

    @pl.when(has_after & is_odd)
    def _():
        for g in range(GROUP):
            send_raw(g).start()

    total = 2 * rows
    keys = 3 * tub * CHUNK
    row = lax.broadcasted_iota(jnp.int32, (total, keys), 0)
    col = lax.broadcasted_iota(jnp.int32, (total, keys), 1)
    step_t = lax.rem(row, rows) // CHUNK
    slot = col // CHUNK
    step_s = lax.rem(slot + tub, 3 * tub)
    same = lax.rem(row, CHUNK) == lax.rem(col, CHUNK)
    valid = same & (step_s >= step_t) & (step_s <= step_t + 2 * tub)
    mask[...] = jnp.where(valid, 1.0, 0.0)


    def normalize(flat):
        embedded = jnp.dot(flat, we[...], preferred_element_type=jnp.float32).astype(jnp.bfloat16)
        wide = embedded.astype(jnp.float32)
        center = wide - jnp.mean(wide, axis=-1, keepdims=True)
        spread = jnp.mean(center * center, axis=-1, keepdims=True)
        scaled = center * lax.rsqrt(spread + 1e-06) * gain[...].reshape(1, width)
        return embedded, scaled.astype(jnp.bfloat16)

    shape4 = (GROUP, tub, CHUNK, half)

    def fill(normed, first, slot):
        for weight, lane in ((wk, 0), (wv, half)):
            part = jnp.dot(normed, weight[...], preferred_element_type=jnp.float32)
            kv[pl.ds(first, GROUP), pl.ds(slot, tub), :, pl.ds(lane, half)] = part.astype(
                jnp.bfloat16
            ).reshape(shape4)

    def project(s, carry):
        first = lax.rem(s + turn, steps) * GROUP
        for g in range(GROUP):
            load_pix(first + g).wait()

        @pl.when(s == 0)
        def _():
            get_we.wait()
            get_gain.wait()

        flat = pix[pl.ds(first, GROUP)].reshape(GROUP * rows, pix.shape[3])
        embedded, normed = normalize(flat)
        emb[pl.ds(first, GROUP)] = embedded.reshape(GROUP, tub, CHUNK, width)

        @pl.when(s == 0)
        def _():
            get_wk.wait()
            get_wv.wait()

        fill(normed, first, own)

        for g in range(GROUP):

            @pl.when(has_after & (is_even | (first > 0)))
            def _():
                send_far(first + g, 0).start()
                send_far(first + g, 1).start()

            @pl.when(is_even)
            def _():
                send_near(first + g, own).start()

        @pl.when(s == 0)
        def _():
            get_wq.wait()

        query = jnp.dot(normed, wq[...], preferred_element_type=jnp.float32).astype(jnp.bfloat16)
        qry[pl.ds(first, GROUP)] = query.reshape(shape4)
        return carry

    lax.fori_loop(0, steps, project, 0)

    @pl.when(has_before & is_odd)
    def _():
        for g in range(GROUP):
            send_raw(g).wait_recv()
        _, normed = normalize(far_pix[...].reshape(GROUP * rows, pix.shape[3]))
        fill(normed, 0, far)

    get_wo.wait()

    @pl.when(me == 0)
    def _():
        def finish(c, carry):
            for which in range(2):
                load_prior(c, which, 0, far, 0).wait()
                load_prior(c, which, tub, near, 1).wait()
            return carry

        lax.fori_loop(0, chunks, finish, 0)

    @pl.when(me == 1)
    def _():
        def finish(c, carry):
            for which in range(2):
                load_prior(c, which, tub, far, 0).wait()
            return carry

        lax.fori_loop(0, chunks, finish, 0)

    scale = 1.0 / math.sqrt(HEAD_DIM)
    window = 2 * LANE
    lane = lax.broadcasted_iota(jnp.int32, (1, window), 1)

    def attend(c, carry):
        @pl.when(has_before & is_odd & (c >= GROUP))
        def _():
            send_far(c, 0).wait_recv()
            send_far(c, 1).wait_recv()

        @pl.when(has_before & is_odd)
        def _():
            send_near(c, far).start()

        @pl.when(has_before | is_odd)
        def _():
            send_near(c, far).wait_recv()

        def score(both, base, slot, size):
            k = kv[c, pl.ds(slot, size), :, pl.ds(base, window)].reshape(size * CHUNK, window)
            found = lax.dot_general(
                both, k, (((1,), (1,)), ((), ())), preferred_element_type=jnp.float32
            )
            seen = mask[:, slot * CHUNK : (slot + size) * CHUNK] > 0.5
            return jnp.where(seen, found * scale, -jnp.inf)

        def blend(weights, base, slot, size):
            v = kv[c, pl.ds(slot, size), :, pl.ds(half + base, window)]
            return jnp.dot(
                weights, v.reshape(size * CHUNK, window), preferred_element_type=jnp.float32
            )

        bases, picks, queries, early = [], [], [], []
        for pair in range(HEADS // 2):
            low = 2 * pair * HEAD_DIM
            base = low // LANE * LANE
            begins = [low + head * HEAD_DIM - base for head in range(2)]
            pick = [
                jnp.where((lane >= begin) & (lane < begin + HEAD_DIM), 1.0, 0.0) for begin in begins
            ]
            q = qry[c, :, :, pl.ds(base, window)].reshape(rows, window)
            both = jnp.concatenate([q * one.astype(jnp.bfloat16) for one in pick], axis=0)
            bases.append(base)
            picks.append(pick)
            queries.append(both)
            early.append(score(both, base, near, 2 * tub))

        @pl.when(has_before & is_even)
        def _():
            send_far(c, 0).wait_recv()

        late, sums = [], []
        for base, both, first in zip(bases, queries, early):
            last = score(both, base, far, tub)
            top = jnp.maximum(
                jnp.max(first, axis=-1, keepdims=True), jnp.max(last, axis=-1, keepdims=True)
            )
            first, last = jnp.exp(first - top), jnp.exp(last - top)
            weight = jnp.sum(first, axis=-1, keepdims=True) + jnp.sum(last, axis=-1, keepdims=True)
            late.append((last / weight).astype(jnp.bfloat16))
            sums.append(blend((first / weight).astype(jnp.bfloat16), base, near, 2 * tub))

        @pl.when(has_before & is_even)
        def _():
            send_far(c, 1).wait_recv()

        tiles = [None] * (half // LANE)
        for base, pick, weights, mixed in zip(bases, picks, late, sums):
            mixed = mixed + blend(weights, base, far, tub)
            part = mixed[:rows] * pick[0] + mixed[rows:] * pick[1]
            for side in range(2):
                piece = part[:, side * LANE : (side + 1) * LANE]
                at = base // LANE + side
                tiles[at] = piece if tiles[at] is None else tiles[at] + piece
        mixed = jnp.concatenate(tiles, axis=1).astype(jnp.bfloat16)
        result = emb[c].reshape(rows, width).astype(jnp.float32) + jnp.dot(
            mixed, wo[...], preferred_element_type=jnp.float32
        )
        encoded[:, patches(c), :] = result.astype(jnp.bfloat16).reshape(tub, CHUNK, width)
        return carry

    lax.fori_loop(0, chunks, attend, 0)

    def drain(c, carry):
        @pl.when(has_after & (is_even | (c >= GROUP)))
        def _():
            send_far(c, 0).wait_send()
            send_far(c, 1).wait_send()

        @pl.when(has_before | is_even)
        def _():
            send_near(c, far).wait_send()

        return carry

    lax.fori_loop(0, chunks, drain, 0)

    @pl.when(has_after & is_odd)
    def _():
        for g in range(GROUP):
            send_raw(g).wait_send()


def body(pixels, prior_kv, w_embed, ln_gain, w_query, w_key, w_value, w_out):
    tub, pat, pix = pixels.shape
    width = w_embed.shape[1]
    half = w_key.shape[1]
    chunks = pat // CHUNK
    bf16 = jnp.bfloat16
    dma = pltpu.SemaphoreType.DMA
    return pl.pallas_call(
        kernel,
        out_shape=pltpu.VMEM((tub, pat, width), bf16),
        in_specs=[pl.BlockSpec(memory_space=pl.ANY)] * 8,
        out_specs=pl.BlockSpec(memory_space=pltpu.VMEM),
        scratch_shapes=[
            pltpu.VMEM((chunks, tub, CHUNK, pix), bf16),
            pltpu.VMEM((GROUP, tub, CHUNK, pix), bf16),
            pltpu.VMEM(w_embed.shape, bf16),
            pltpu.VMEM((width,), jnp.float32),
            pltpu.VMEM(w_query.shape, bf16),
            pltpu.VMEM(w_key.shape, bf16),
            pltpu.VMEM(w_value.shape, bf16),
            pltpu.VMEM(w_out.shape, bf16),
            pltpu.VMEM((chunks, tub, CHUNK, width), bf16),
            pltpu.VMEM((chunks, tub, CHUNK, half), bf16),
            pltpu.VMEM((chunks, 3 * tub, CHUNK, 2 * half), bf16),
            pltpu.VMEM((2 * tub * CHUNK, 3 * tub * CHUNK), jnp.float32),
            dma((6,)),
            dma((chunks,)),
            dma((2, 2, chunks)),
            dma((2, chunks)),
            dma((2, chunks)),
            dma((chunks,)),
            dma((chunks,)),
            dma((GROUP,)),
            dma((GROUP,)),
        ],
        compiler_params=pltpu.CompilerParams(collective_id=0, has_side_effects=True, vmem_limit_bytes=65500000),
    )(pixels, prior_kv, w_embed, ln_gain, w_query, w_key, w_value, w_out)


def solution(mesh):
    placed = (
        P(("groups", "tm"), None, None),
        P(None, "groups", None, None),
        P(),
        P(),
        P(),
        P(),
        P(),
        P(),
    )
    return jax.shard_map(
        body, mesh=mesh, in_specs=placed, out_specs=P(("groups", "tm"), None, None), check_vma=False
    )
```

```python
import functools
import math

import jax
import jax.numpy as jnp
from jax import lax
from jax.experimental import pallas as pl
from jax.experimental.pallas import tpu as pltpu
from jax.sharding import PartitionSpec as P

HEADS = 8
HEAD_DIM = 80
LANE = 128
CHUNK = 16
GROUP = 2
MESH = pl.DeviceIdType.MESH


def kernel(
    pixels,
    prior,
    w_embed,
    ln_gain,
    w_query,
    w_key,
    w_value,
    w_out,
    encoded,
    pix,
    far_pix,
    we,
    gain,
    wq,
    wk,
    wv,
    wo,
    emb,
    qry,
    kv,
    mask,
    w_sem,
    pix_sem,
    prior_sem,
    far_send,
    far_recv,
    near_send,
    near_recv,
    raw_send,
    raw_recv,
):
    count = lax.axis_size("tm")
    me = lax.axis_index("tm")
    tub = pixels.shape[0]
    chunks = pixels.shape[1] // CHUNK
    half = kv.shape[3] // 2
    width = emb.shape[3]
    rows = tub * CHUNK
    near, own, far = 0, tub, 2 * tub
    is_even = lax.rem(me, 2) == 0
    is_odd = jnp.logical_not(is_even)
    partner = jnp.where(is_even, me + 1, me - 1)
    has_before = me >= 2
    steps = chunks // GROUP
    turn = lax.rem(me, 2)
    has_after = me + 2 < count

    barrier = pltpu.get_barrier_semaphore()
    pl.semaphore_signal(barrier, inc=1, device_id={"tm": partner}, device_id_type=MESH)

    @pl.when(has_before)
    def _():
        pl.semaphore_signal(barrier, inc=1, device_id={"tm": me - 2}, device_id_type=MESH)

    @pl.when(has_after)
    def _():
        pl.semaphore_signal(barrier, inc=1, device_id={"tm": me + 2}, device_id_type=MESH)

    def patches(c):
        return pl.ds(pl.multiple_of(c * CHUNK, CHUNK), CHUNK)

    def load_pix(c):
        return pltpu.make_async_copy(pixels.at[:, patches(c), :], pix.at[c], pix_sem.at[c])

    def load_weight(source, target, index):
        return pltpu.make_async_copy(source, target, w_sem.at[index])

    get_we = load_weight(w_embed, we, 0)
    get_gain = load_weight(ln_gain, gain, 1)
    get_wk = load_weight(w_key, wk, 2)
    get_wv = load_weight(w_value, wv, 3)
    get_wq = load_weight(w_query, wq, 4)
    get_wo = load_weight(w_out, wo, 5)

    def load_prior(c, which, first, slot, index):
        return pltpu.make_async_copy(
            prior.at[which, pl.ds(first, tub), patches(c), :],
            kv.at[c, pl.ds(slot, tub), :, pl.ds(which * half, half)],
            prior_sem.at[index, which, c],
        )

    def send_far(c, which):
        lanes = pl.ds(which * half, half)
        return pltpu.make_async_remote_copy(
            src_ref=kv.at[c, pl.ds(own, tub), :, lanes],
            dst_ref=kv.at[c, pl.ds(far, tub), :, lanes],
            send_sem=far_send.at[which, c],
            recv_sem=far_recv.at[which, c],
            device_id={"tm": me + 2},
            device_id_type=MESH,
        )

    def send_raw(g):
        return pltpu.make_async_remote_copy(
            src_ref=pixels.at[:, patches(g), :],
            dst_ref=far_pix.at[g],
            send_sem=raw_send.at[g],
            recv_sem=raw_recv.at[g],
            device_id={"tm": me + 2},
            device_id_type=MESH,
        )

    def send_near(c, slot):
        return pltpu.make_async_remote_copy(
            src_ref=kv.at[c, pl.ds(slot, tub)],
            dst_ref=kv.at[c, pl.ds(near, tub)],
            send_sem=near_send.at[c],
            recv_sem=near_recv.at[c],
            device_id={"tm": partner},
            device_id_type=MESH,
        )

    for g in range(GROUP):
        load_pix(lax.rem(turn, steps) * GROUP + g).start()
    get_we.start()
    get_gain.start()
    get_wk.start()
    get_wv.start()
    get_wq.start()
    for s in range(1, steps):
        for g in range(GROUP):
            load_pix(lax.rem(s + turn, steps) * GROUP + g).start()
    get_wo.start()

    @pl.when(me == 0)
    def _():
        def start(c, carry):
            for which in range(2):
                load_prior(c, which, 0, far, 0).start()
                load_prior(c, which, tub, near, 1).start()
            return carry

        lax.fori_loop(0, chunks, start, 0)

    @pl.when(me == 1)
    def _():
        def start(c, carry):
            for which in range(2):
                load_prior(c, which, tub, far, 0).start()
            return carry

        lax.fori_loop(0, chunks, start, 0)

    expected = 1 + has_before.astype(jnp.int32) + has_after.astype(jnp.int32)
    pl.semaphore_wait(barrier, expected)

    @pl.when(has_after & is_odd)
    def _():
        for g in range(GROUP):
            send_raw(g).start()

    def normalize(flat):
        embedded = jnp.dot(flat, we[...], preferred_element_type=jnp.float32).astype(jnp.bfloat16)
        wide = embedded.astype(jnp.float32)
        center = wide - jnp.mean(wide, axis=-1, keepdims=True)
        spread = jnp.mean(center * center, axis=-1, keepdims=True)
        scaled = center * lax.rsqrt(spread + 1e-06) * gain[...].reshape(1, width)
        return embedded, scaled.astype(jnp.bfloat16)

    shape4 = (GROUP, tub, CHUNK, half)

    def fill(normed, first, slot):
        for weight, lane in ((wk, 0), (wv, half)):
            part = jnp.dot(normed, weight[...], preferred_element_type=jnp.float32)
            kv[pl.ds(first, GROUP), pl.ds(slot, tub), :, pl.ds(lane, half)] = part.astype(
                jnp.bfloat16
            ).reshape(shape4)

    def project(s, carry):
        first = lax.rem(s + turn, steps) * GROUP
        for g in range(GROUP):
            load_pix(first + g).wait()

        @pl.when(s == 0)
        def _():
            get_we.wait()
            get_gain.wait()

        flat = pix[pl.ds(first, GROUP)].reshape(GROUP * rows, pix.shape[3])
        embedded, normed = normalize(flat)
        emb[pl.ds(first, GROUP)] = embedded.reshape(GROUP, tub, CHUNK, width)

        @pl.when(s == 0)
        def _():
            get_wk.wait()
            get_wv.wait()

        fill(normed, first, own)

        for g in range(GROUP):

            @pl.when(has_after & (is_even | (first > 0)))
            def _():
                send_far(first + g, 0).start()
                send_far(first + g, 1).start()

            @pl.when(is_even)
            def _():
                send_near(first + g, own).start()

        @pl.when(s == 0)
        def _():
            get_wq.wait()

        query = jnp.dot(normed, wq[...], preferred_element_type=jnp.float32).astype(jnp.bfloat16)
        qry[pl.ds(first, GROUP)] = query.reshape(shape4)
        return carry

    lax.fori_loop(0, steps, project, 0)
    total = 2 * rows
    keys = 3 * tub * CHUNK
    row = lax.broadcasted_iota(jnp.int32, (total, keys), 0)
    col = lax.broadcasted_iota(jnp.int32, (total, keys), 1)
    step_t = lax.rem(row, rows) // CHUNK
    slot = col // CHUNK
    step_s = lax.rem(slot + tub, 3 * tub)
    same = lax.rem(row, CHUNK) == lax.rem(col, CHUNK)
    valid = same & (step_s >= step_t) & (step_s <= step_t + 2 * tub)
    mask[...] = jnp.where(valid, 1.0, 0.0)


    @pl.when(has_before & is_odd)
    def _():
        for g in range(GROUP):
            send_raw(g).wait_recv()
        _, normed = normalize(far_pix[...].reshape(GROUP * rows, pix.shape[3]))
        fill(normed, 0, far)

    get_wo.wait()

    @pl.when(me == 0)
    def _():
        def finish(c, carry):
            for which in range(2):
                load_prior(c, which, 0, far, 0).wait()
                load_prior(c, which, tub, near, 1).wait()
            return carry

        lax.fori_loop(0, chunks, finish, 0)

    @pl.when(me == 1)
    def _():
        def finish(c, carry):
            for which in range(2):
                load_prior(c, which, tub, far, 0).wait()
            return carry

        lax.fori_loop(0, chunks, finish, 0)

    scale = 1.0 / math.sqrt(HEAD_DIM)
    window = 2 * LANE
    lane = lax.broadcasted_iota(jnp.int32, (1, window), 1)

    def attend(c, carry):
        @pl.when(has_before & is_odd & (c >= GROUP))
        def _():
            send_far(c, 0).wait_recv()
            send_far(c, 1).wait_recv()

        @pl.when(has_before & is_odd)
        def _():
            send_near(c, far).start()

        @pl.when(has_before | is_odd)
        def _():
            send_near(c, far).wait_recv()

        def score(both, base, slot, size):
            k = kv[c, pl.ds(slot, size), :, pl.ds(base, window)].reshape(size * CHUNK, window)
            found = lax.dot_general(
                both, k, (((1,), (1,)), ((), ())), preferred_element_type=jnp.float32
            )
            seen = mask[:, slot * CHUNK : (slot + size) * CHUNK] > 0.5
            return jnp.where(seen, found * scale, -jnp.inf)

        def blend(weights, base, slot, size):
            v = kv[c, pl.ds(slot, size), :, pl.ds(half + base, window)]
            return jnp.dot(
                weights, v.reshape(size * CHUNK, window), preferred_element_type=jnp.float32
            )

        bases, picks, queries, early = [], [], [], []
        for pair in range(HEADS // 2):
            low = 2 * pair * HEAD_DIM
            base = low // LANE * LANE
            begins = [low + head * HEAD_DIM - base for head in range(2)]
            pick = [
                jnp.where((lane >= begin) & (lane < begin + HEAD_DIM), 1.0, 0.0) for begin in begins
            ]
            q = qry[c, :, :, pl.ds(base, window)].reshape(rows, window)
            both = jnp.concatenate([q * one.astype(jnp.bfloat16) for one in pick], axis=0)
            bases.append(base)
            picks.append(pick)
            queries.append(both)
            early.append(score(both, base, near, 2 * tub))

        @pl.when(has_before & is_even)
        def _():
            send_far(c, 0).wait_recv()

        late, sums = [], []
        for base, both, first in zip(bases, queries, early):
            last = score(both, base, far, tub)
            top = jnp.maximum(
                jnp.max(first, axis=-1, keepdims=True), jnp.max(last, axis=-1, keepdims=True)
            )
            first, last = jnp.exp(first - top), jnp.exp(last - top)
            weight = jnp.sum(first, axis=-1, keepdims=True) + jnp.sum(last, axis=-1, keepdims=True)
            late.append((last / weight).astype(jnp.bfloat16))
            sums.append(blend((first / weight).astype(jnp.bfloat16), base, near, 2 * tub))

        @pl.when(has_before & is_even)
        def _():
            send_far(c, 1).wait_recv()

        tiles = [None] * (half // LANE)
        for base, pick, weights, mixed in zip(bases, picks, late, sums):
            mixed = mixed + blend(weights, base, far, tub)
            part = mixed[:rows] * pick[0] + mixed[rows:] * pick[1]
            for side in range(2):
                piece = part[:, side * LANE : (side + 1) * LANE]
                at = base // LANE + side
                tiles[at] = piece if tiles[at] is None else tiles[at] + piece
        mixed = jnp.concatenate(tiles, axis=1).astype(jnp.bfloat16)
        result = emb[c].reshape(rows, width).astype(jnp.float32) + jnp.dot(
            mixed, wo[...], preferred_element_type=jnp.float32
        )
        encoded[:, patches(c), :] = result.astype(jnp.bfloat16).reshape(tub, CHUNK, width)
        return carry

    lax.fori_loop(0, chunks, attend, 0)

    def drain(c, carry):
        @pl.when(has_after & (is_even | (c >= GROUP)))
        def _():
            send_far(c, 0).wait_send()
            send_far(c, 1).wait_send()

        @pl.when(has_before | is_even)
        def _():
            send_near(c, far).wait_send()

        return carry

    lax.fori_loop(0, chunks, drain, 0)

    @pl.when(has_after & is_odd)
    def _():
        for g in range(GROUP):
            send_raw(g).wait_send()


def body(pixels, prior_kv, w_embed, ln_gain, w_query, w_key, w_value, w_out):
    tub, pat, pix = pixels.shape
    width = w_embed.shape[1]
    half = w_key.shape[1]
    chunks = pat // CHUNK
    bf16 = jnp.bfloat16
    dma = pltpu.SemaphoreType.DMA
    return pl.pallas_call(
        kernel,
        out_shape=pltpu.VMEM((tub, pat, width), bf16),
        in_specs=[pl.BlockSpec(memory_space=pl.ANY)] * 8,
        out_specs=pl.BlockSpec(memory_space=pltpu.VMEM),
        scratch_shapes=[
            pltpu.VMEM((chunks, tub, CHUNK, pix), bf16),
            pltpu.VMEM((GROUP, tub, CHUNK, pix), bf16),
            pltpu.VMEM(w_embed.shape, bf16),
            pltpu.VMEM((width,), jnp.float32),
            pltpu.VMEM(w_query.shape, bf16),
            pltpu.VMEM(w_key.shape, bf16),
            pltpu.VMEM(w_value.shape, bf16),
            pltpu.VMEM(w_out.shape, bf16),
            pltpu.VMEM((chunks, tub, CHUNK, width), bf16),
            pltpu.VMEM((chunks, tub, CHUNK, half), bf16),
            pltpu.VMEM((chunks, 3 * tub, CHUNK, 2 * half), bf16),
            pltpu.VMEM((2 * tub * CHUNK, 3 * tub * CHUNK), jnp.float32),
            dma((6,)),
            dma((chunks,)),
            dma((2, 2, chunks)),
            dma((2, chunks)),
            dma((2, chunks)),
            dma((chunks,)),
            dma((chunks,)),
            dma((GROUP,)),
            dma((GROUP,)),
        ],
        compiler_params=pltpu.CompilerParams(collective_id=0, has_side_effects=True, vmem_limit_bytes=65500000),
    )(pixels, prior_kv, w_embed, ln_gain, w_query, w_key, w_value, w_out)


def solution(mesh):
    placed = (
        P(("groups", "tm"), None, None),
        P(None, "groups", None, None),
        P(),
        P(),
        P(),
        P(),
        P(),
        P(),
    )
    return jax.shard_map(
        body, mesh=mesh, in_specs=placed, out_specs=P(("groups", "tm"), None, None), check_vma=False
    )
```
